32 devices in a mesh: section: 4 (over y, core), seq: 8 (over z, x).
Axes of the slice: x: 2, y: 2, z: 4, core: 2. Of those that a mesh axis runs over, the one named last changes fastest.
Arguments:
- context: bfloat16 [2048, 8192], P('seq'), may hold values from -24 to 24, as said below
- memory: bfloat16 [512, 8192], P('seq'), may hold values from -24 to 24, as said below
- query_weight: bfloat16 [8192, 4096], P(None, 'section'), may hold values from -0.0625 to 0.0625
- key_weight: bfloat16 [8192, 512], P('seq', 'section'), may hold values from -0.0625 to 0.0625
- value_weight: bfloat16 [8192, 512], P('seq', 'section'), may hold values from -0.0625 to 0.0625
- query_down_map: bfloat16 [8192, 128], replicated, may hold values from -0.0625 to 0.0625
- query_up_map: bfloat16 [128, 4096], P(None, 'section'), may hold values from -0.5 to 0.5
- value_down_map: bfloat16 [8192, 128], P('seq'), may hold values from -0.0625 to 0.0625
- value_up_map: bfloat16 [128, 512], P(None, 'section'), may hold values from -0.5 to 0.5
- output_weight: bfloat16 [4096, 8192], P('section', 'seq'), may hold values from -1 to 1
- decoder_gain: float32 [8192], P('seq'), may hold values from 0.25 to 1.75
- document_slots: int32 [8], replicated, may hold values from 1 to 320, 512 in all
- normed_gradient: bfloat16 [512, 8192], P('section', 'seq'), may hold values from -6 to 6
Outputs:
- normed: bfloat16 [512, 8192], P('section', 'seq')
- grad_qa: float32 [8192, 128], P(('section', 'seq'))
- grad_va: float32 [8192, 128], P(('section', 'seq'))
- query_up_gradient: float32 [128, 4096], P(None, 'section')
- value_up_gradient: float32 [128, 512], P(None, 'section')
The draws below stay inside these ranges and needn't reach their ends.
Inputs may be any that keep to these rules, and one draw needn't show every extreme that they name: `context`: values of the normed inputs lie in this range. `memory`: values of the normed inputs lie in this range. Documents lie end to end in order; document d has document_slots[d] memory slots and 4 document_slots[d] context tokens; the counts sum to 512.
All inputs are finite; a program needn't handle non-finite values.
Results may differ from the reference program's by a relative error of at most 0.014.
The reference program's roundings to bfloat16 on the way count: a program that leaves them out, or rounds other values in their place, can miss the bound.
Values may be sent and summed in bfloat16 or wider, within the bound.
No kernel may reach another device: no remote copies, remote signals or barrier semaphores. Data moves between devices by JAX's collectives and lax.ppermute only.
A program may use at most 192 MiB of HBM per device.

```python
import math
import jax
import jax.numpy as jnp
import numpy as np
from jax import lax

MODEL_DIM = 8192
HEADS = 32
KV_HEADS = 4
HD = 128
ADAPTER_RANK = 128
DOCS = 8
SLOT_DEV = 64
LEN = 2048
SLOTS = 512
KEYS = 2560
QUERY_FEATURES = 4096
KEY_FEATURES = 512


def input_rows(key, row_total):
    base = jnp.clip(jax.random.normal(jax.random.fold_in(key, 11), (row_total, MODEL_DIM), jnp.float32), -4.0, 4.0)
    return base


def draw_context(key, part):
    return input_rows(jax.random.fold_in(key, 21), LEN).astype(jnp.bfloat16)


def draw_memory(key, part):
    return input_rows(jax.random.fold_in(key, 22), SLOTS).astype(jnp.bfloat16)


def draw_output_weight(key, part):
    ramp = 0.6 + 1.2 * jnp.arange(MODEL_DIM, dtype=jnp.float32) / MODEL_DIM
    base = jnp.clip(jax.random.normal(jax.random.fold_in(key, 32), (QUERY_FEATURES, MODEL_DIM), jnp.float32), -4.0, 4.0)
    return jnp.clip(base * ramp[None, :] * QUERY_FEATURES ** (-0.5), -1.0, 1.0).astype(jnp.bfloat16)


def raised(entries, key, source, target, blocks, factor):
    owner, partner = [(jnp.arange(entries.shape[position]) // (entries.shape[position] // blocks)).reshape([-1 if axis == position else 1 for axis in range(entries.ndim)]) for position in (source, target)]
    chosen = jax.random.permutation(key, blocks)[partner]
    strong = (owner == chosen) | (owner == (partner + blocks // 2) % blocks)
    return jnp.where(strong, factor * entries, entries)


def levels(key, extent, split, smallest, top_value):
    level = 1.0
    for dim, shards_of in split:
        heights = jax.random.uniform(jax.random.fold_in(jax.random.fold_in(key, 6), dim), (shards_of,), jnp.float32, smallest / len(split), top_value / len(split))
        level = level * jnp.repeat(jnp.exp(heights), extent[dim] // shards_of).reshape((-1,) + (1,) * (len(extent) - 1 - dim))
    return level


def length_profile(amount, total, limit, lean):
    loads = [(1 << 20) // math.isqrt(rank ** lean) + 1 for rank in range(2, amount + 1)]
    spare, holding = total - limit - (amount - 1), [1] * (amount - 1)
    while spare > 0:
        free = [i for i in range(amount - 1) if holding[i] < limit]
        mass, budget = sum([loads[i] for i in free]), spare
        for i in free:
            addition = min(limit - holding[i], max(1, budget * loads[i] // mass), spare)
            holding[i] = holding[i] + addition
            spare = spare - addition
    return np.array([limit] + holding)


def ragged_sizes(rng, count, total, most, slope):
    if count == 2:
        one = jax.random.randint(rng, (), max(1, total - most), min(most, total - 1) + 1)
        return jnp.stack([one, total - one])
    lengths = jnp.asarray(length_profile(count, total, most, slope), jnp.int32)
    twos = (count - 1) // 2
    donor, taker = lengths[1:1 + 2 * twos:2], lengths[2:2 + 2 * twos:2]
    margin = jnp.minimum(donor - 1, most - taker)
    shifted = jax.random.randint(jax.random.fold_in(rng, 1), (twos,), 0, 1 << 20) % (margin + 1)
    lengths = lengths.at[1:1 + 2 * twos:2].set(donor - shifted).at[2:2 + 2 * twos:2].set(taker + shifted)
    return lengths[jax.random.permutation(jax.random.fold_in(rng, 2), count)]


def normal_values(key, extent, width, reach, pieces=(), held_as=jnp.bfloat16):
    array = width * jax.random.normal(key, extent, jnp.float32)
    if pieces:
        array = array * levels(key, extent, pieces, -0.22, 0.18)
    return jnp.clip(array, -reach, reach).astype(held_as)


def gaussian_with(stream_key, extent, deviation, limit, split, heavy, kind=jnp.bfloat16):
    result = deviation * jax.random.normal(stream_key, extent, jnp.float32)
    if split:
        result = result * levels(stream_key, extent, split, -0.22, 0.18)
    return jnp.clip(raised(result, jax.random.fold_in(stream_key, 3), *heavy), -limit, limit).astype(kind)


def setup_inputs(seed: int = 0) -> dict:
    key_of = jax.random.split(jax.random.key(seed), 14)
    return {
        "context": draw_context(jax.random.fold_in(key_of[13], 71), 0),
        "memory": draw_memory(jax.random.fold_in(key_of[13], 71), 0),
        "query_weight": normal_values(key_of[2], (MODEL_DIM, QUERY_FEATURES), MODEL_DIM ** -0.5, 0.0625, ((1, 4),)),
        "key_weight": normal_values(key_of[3], (MODEL_DIM, KEY_FEATURES), MODEL_DIM ** -0.5, 0.0625, ((0, 8), (1, 4))),
        "value_weight": normal_values(key_of[4], (MODEL_DIM, KEY_FEATURES), MODEL_DIM ** -0.5, 0.0625, ((0, 8), (1, 4))),
        "query_down_map": normal_values(key_of[5], (MODEL_DIM, ADAPTER_RANK), MODEL_DIM ** -0.5, 0.0625),
        "query_up_map": normal_values(key_of[6], (ADAPTER_RANK, QUERY_FEATURES), ADAPTER_RANK ** -0.5, 0.5, ((1, 4),)),
        "value_down_map": normal_values(key_of[7], (MODEL_DIM, ADAPTER_RANK), MODEL_DIM ** -0.5, 0.0625, ((0, 8),)),
        "value_up_map": normal_values(key_of[8], (ADAPTER_RANK, KEY_FEATURES), ADAPTER_RANK ** -0.5, 0.5, ((1, 4),)),
        "output_weight": draw_output_weight(jax.random.fold_in(key_of[13], 71), 0),
        "decoder_gain": jnp.clip(1.0 + 0.15 * jax.random.normal(key_of[10], (MODEL_DIM,), jnp.float32), 0.25, 1.75),
        "document_slots": ragged_sizes(key_of[11], DOCS, SLOTS, SLOTS // 2 + SLOT_DEV, 2).astype(jnp.int32),
        "normed_gradient": gaussian_with(key_of[12], (SLOTS, MODEL_DIM), 1.0, 6.0, ((0, 4), (1, 8)), (1, 0, 8, 2.0)),
    }


adapter_scale = 0.25
epsilon = 1e-05
mask_fill = -1e+30

def doc_index(units, doc_ends):
    return lax.optimization_barrier(jnp.sum((units[:, None] >= doc_ends[None, :]).astype(jnp.int32), axis=1)).astype(jnp.int32)

def block_probs(query_block, keys_head, slot_unit, key_unit, key_doc, is_context, doc_ends, group_heads):
    query_rows = query_block.reshape(-1, HD)
    row_unit = jnp.repeat(slot_unit, group_heads)
    row_doc = doc_index(row_unit, doc_ends)
    allowed = (key_doc[None, :] == row_doc[:, None]) & (is_context[None, :] | (key_unit[None, :] <= row_unit[:, None]))
    scores = jnp.dot(query_rows, keys_head.T, preferred_element_type=jnp.float32) * HD ** (-0.5)
    scores = jnp.where(allowed, scores, mask_fill)
    row_top = lax.optimization_barrier(jnp.max(scores, axis=1, keepdims=True))
    exponent = jnp.exp(scores - row_top)
    return exponent / lax.optimization_barrier(jnp.sum(exponent, axis=1, keepdims=True))

def reference(context, memory, query_weight, key_weight, value_weight, query_down_map, query_up_map, value_down_map, value_up_map, output_weight, decoder_gain, document_slots, normed_gradient):
    doc_ends = jnp.cumsum(document_slots).astype(jnp.int32)
    every_row = jnp.concatenate([context, memory], axis=0)
    query_reduced = jnp.dot(memory, query_down_map, preferred_element_type=jnp.float32).astype(jnp.bfloat16)
    value_reduced = jnp.dot(every_row, value_down_map, preferred_element_type=jnp.float32).astype(jnp.bfloat16)
    query_rows_out = (jnp.dot(memory, query_weight, preferred_element_type=jnp.float32) + adapter_scale * jnp.dot(query_reduced, query_up_map, preferred_element_type=jnp.float32)).astype(jnp.bfloat16)
    keys_all = jnp.dot(every_row, key_weight, preferred_element_type=jnp.float32).astype(jnp.bfloat16)
    value_rows_all = (jnp.dot(every_row, value_weight, preferred_element_type=jnp.float32) + adapter_scale * jnp.dot(value_reduced, value_up_map, preferred_element_type=jnp.float32)).astype(jnp.bfloat16)
    key_unit = jnp.concatenate([jnp.arange(LEN, dtype=jnp.int32) // 4, jnp.arange(SLOTS, dtype=jnp.int32)])
    is_context = jnp.concatenate([jnp.ones((LEN,), dtype=bool), jnp.zeros((SLOTS,), dtype=bool)])
    key_doc = doc_index(key_unit, doc_ends)
    group_heads = HEADS // KV_HEADS
    group_width = group_heads * HD
    slot_block = SLOT_DEV
    block_total = SLOTS // slot_block

    def forward_head(head_index):
        query_head = lax.dynamic_slice_in_dim(query_rows_out, head_index * group_width, group_width, 1)
        keys_head = lax.dynamic_slice_in_dim(keys_all, head_index * HD, HD, 1)
        values_head = lax.dynamic_slice_in_dim(value_rows_all, head_index * HD, HD, 1)

        def per_block(block_index):
            begin_row = block_index * slot_block
            query_block = lax.dynamic_slice_in_dim(query_head, begin_row, slot_block, 0)
            slot_unit = begin_row + jnp.arange(slot_block, dtype=jnp.int32)
            probs = block_probs(query_block, keys_head, slot_unit, key_unit, key_doc, is_context, doc_ends, group_heads)
            output = jnp.dot(probs.astype(jnp.bfloat16), values_head, preferred_element_type=jnp.float32)
            return output.reshape(slot_block, group_width).astype(jnp.bfloat16)
        return lax.map(per_block, jnp.arange(block_total, dtype=jnp.int32)).reshape(SLOTS, group_width)
    attended = lax.map(forward_head, jnp.arange(KV_HEADS, dtype=jnp.int32))
    attended = jnp.transpose(attended, (1, 0, 2)).reshape(SLOTS, QUERY_FEATURES)
    hidden = jnp.dot(attended, output_weight, preferred_element_type=jnp.float32)
    inv_rms = lax.rsqrt(lax.optimization_barrier(jnp.mean(hidden * hidden, axis=1)) + epsilon)
    normed = (hidden * inv_rms[:, None] * decoder_gain).astype(jnp.bfloat16)
    weighted = SLOTS ** (-0.5) * normed_gradient.astype(jnp.float32) * decoder_gain
    cross = lax.optimization_barrier(jnp.sum(weighted * hidden, axis=1))
    d_hidden = (inv_rms[:, None] * weighted - hidden * (inv_rms ** 3 * cross / MODEL_DIM)[:, None]).astype(jnp.bfloat16)
    d_attended = jnp.dot(d_hidden, output_weight.T, preferred_element_type=jnp.float32).astype(jnp.bfloat16)

    def backward_head(head_index):
        query_head = lax.dynamic_slice_in_dim(query_rows_out, head_index * group_width, group_width, 1)
        grad_head = lax.dynamic_slice_in_dim(d_attended, head_index * group_width, group_width, 1)
        keys_head = lax.dynamic_slice_in_dim(keys_all, head_index * HD, HD, 1)
        values_head = lax.dynamic_slice_in_dim(value_rows_all, head_index * HD, HD, 1)

        def per_block(value_sum, block_index):
            begin_row = block_index * slot_block
            query_block = lax.dynamic_slice_in_dim(query_head, begin_row, slot_block, 0)
            grad_block = lax.dynamic_slice_in_dim(grad_head, begin_row, slot_block, 0).reshape(-1, HD)
            slot_unit = begin_row + jnp.arange(slot_block, dtype=jnp.int32)
            probs = block_probs(query_block, keys_head, slot_unit, key_unit, key_doc, is_context, doc_ends, group_heads)
            d_probs = jnp.dot(grad_block, values_head.T, preferred_element_type=jnp.float32)
            center = lax.optimization_barrier(jnp.sum(probs * d_probs, axis=1, keepdims=True))
            d_scores = (probs * (d_probs - center)).astype(jnp.bfloat16)
            d_query = (HD ** (-0.5) * jnp.dot(d_scores, keys_head, preferred_element_type=jnp.float32)).reshape(slot_block, group_width).astype(jnp.bfloat16)
            value_sum = value_sum + jnp.dot(probs.astype(jnp.bfloat16).T, grad_block, preferred_element_type=jnp.float32)
            return (value_sum, d_query)
        value_sum, query_blocks = lax.scan(per_block, jnp.zeros((KEYS, HD), jnp.float32), jnp.arange(block_total, dtype=jnp.int32))
        return (query_blocks.reshape(SLOTS, group_width), value_sum.astype(jnp.bfloat16))
    query_parts, value_parts = lax.map(backward_head, jnp.arange(KV_HEADS, dtype=jnp.int32))
    query_gradient = jnp.transpose(query_parts, (1, 0, 2)).reshape(SLOTS, QUERY_FEATURES)
    value_gradient = jnp.transpose(value_parts, (1, 0, 2)).reshape(KEYS, KEY_FEATURES)
    query_up_gradient = adapter_scale * jnp.dot(query_reduced.T, query_gradient, preferred_element_type=jnp.float32)
    value_up_gradient = adapter_scale * jnp.dot(value_reduced.T, value_gradient, preferred_element_type=jnp.float32)
    query_backward = (adapter_scale * jnp.dot(query_gradient, query_up_map.T, preferred_element_type=jnp.float32)).astype(jnp.bfloat16)
    value_backward = (adapter_scale * jnp.dot(value_gradient, value_up_map.T, preferred_element_type=jnp.float32)).astype(jnp.bfloat16)
    grad_qa = jnp.dot(memory.T, query_backward, preferred_element_type=jnp.float32)
    grad_va = jnp.dot(every_row.T, value_backward, preferred_element_type=jnp.float32)
    return (normed, grad_qa, grad_va, query_up_gradient, value_up_gradient)
```

```python
import jax
import jax.numpy as jnp
from jax import lax
from jax.sharding import PartitionSpec as P


adapter_scale = 0.25
epsilon = 1e-05
mask_fill = -1e30


def doc_index(units, doc_ends):
    return jnp.sum((units[:, None] >= doc_ends[None, :]).astype(jnp.int32), axis=1)


def leading_contract(left, right):
    return lax.dot_general(
        left, right, (((0,), (0,)), ((), ())), preferred_element_type=jnp.float32
    )


def trailing_contract(left, right):
    return lax.dot_general(
        left, right, (((1,), (1,)), ((), ())), preferred_element_type=jnp.float32
    )


def swap(x, axis, bits):
    size = lax.axis_size(axis)
    return lax.ppermute(x, axis, [(i, i ^ bits) for i in range(size)])


def gather_blocks(x, axis="seq"):
    size = lax.axis_size(axis)
    blocks = [x] + [None] * (size - 1)
    for far in reversed(range(2, size, 2)):
        blocks[far] = swap(x, axis, far)
    for far in range(0, size, 2):
        blocks[far + 1] = swap(blocks[far], axis, 1)
    return blocks


def scatter_sum(parts, axis="seq", wire=jnp.bfloat16):
    size = lax.axis_size(axis)
    sums = [None] * size
    for far in reversed(range(0, size, 2)):
        sums[far] = parts[far] + swap(parts[far + 1].astype(wire), axis, 1).astype(jnp.float32)
    total = sums[0]
    for far in reversed(range(2, size, 2)):
        total = total + swap(sums[far].astype(wire), axis, far).astype(jnp.float32)
    return total


def in_order(blocks, index):
    blocks = list(blocks)
    bit = 1
    while bit < len(blocks):
        flip = (index & bit) != 0
        blocks = [jnp.where(flip, blocks[k ^ bit], blocks[k]) for k in range(len(blocks))]
        bit *= 2
    return blocks


def section_sum(x, wire=jnp.bfloat16):
    low = x.astype(wire)
    total = x
    for bits in reversed(range(1, lax.axis_size("section"))):
        total = total + swap(low, "section", bits).astype(jnp.float32)
    return total


def body(
    context,
    memory,
    query_weight,
    key_weight,
    value_weight,
    query_down_map,
    query_up_map,
    value_down_map,
    value_up_map,
    output_weight,
    decoder_gain,
    document_slots,
    normed_gradient,
):
    tok_dev = context.shape[0]
    slot_dev = memory.shape[0]
    keys_dev = tok_dev + slot_dev
    model_width = memory.shape[1]
    seq_size = lax.axis_size("seq")
    seq_index = lax.axis_index("seq")
    section_extent = lax.axis_size("section")
    section_index = lax.axis_index("section")
    head_dim = key_weight.shape[1]
    group_heads = query_weight.shape[1] // head_dim
    chunk = key_weight.shape[0]
    rank = value_down_map.shape[1]
    rank_part = rank // section_extent

    down_part = lax.dynamic_slice_in_dim(
        value_down_map, section_index * rank_part, rank_part, 1
    ).T
    down_blocks = gather_blocks(down_part)
    key_blocks = gather_blocks(key_weight)
    value_blocks = gather_blocks(value_weight)

    query_reduced = jnp.dot(memory, query_down_map, preferred_element_type=jnp.float32).astype(
        jnp.bfloat16
    )
    query_rows_out = (
        jnp.dot(memory, query_weight, preferred_element_type=jnp.float32)
        + adapter_scale * jnp.dot(query_reduced, query_up_map, preferred_element_type=jnp.float32)
    ).astype(jnp.bfloat16)
    query_reduced_all = jnp.concatenate(in_order(gather_blocks(query_reduced), seq_index), axis=0)

    gradient_pair = [normed_gradient, swap(normed_gradient, "section", 1)]
    gradient_blocks = gradient_pair + [
        swap(g, "section", far) for far in range(2, section_extent, 2) for g in gradient_pair
    ]
    gradient_all = jnp.concatenate(in_order(gradient_blocks, section_index), axis=0)
    gradient_rows = jnp.concatenate(
        [
            lax.dynamic_slice_in_dim(gradient_all, (seq_index ^ k) * slot_dev, slot_dev, 0)
            for k in range(seq_size)
        ],
        axis=0,
    )

    row_chunks = [
        jnp.concatenate(
            [
                lax.dynamic_slice_in_dim(context, (seq_index ^ k) * chunk, chunk, 1),
                lax.dynamic_slice_in_dim(memory, (seq_index ^ k) * chunk, chunk, 1),
            ],
            axis=0,
        )
        for k in range(seq_size)
    ]
    reduced_part = sum(
        trailing_contract(r, w) for r, w in zip(row_chunks, down_blocks)
    ).astype(jnp.bfloat16)
    reduced_parts = [reduced_part] + [
        swap(reduced_part, "section", bits) for bits in range(1, section_extent)
    ]
    value_reduced = jnp.concatenate(in_order(reduced_parts, section_index), axis=1)
    keys_local = sum(
        jnp.dot(r, w, preferred_element_type=jnp.float32) for r, w in zip(row_chunks, key_blocks)
    ).astype(jnp.bfloat16)
    keys_all = jnp.concatenate(gather_blocks(keys_local), axis=0)
    values_local = (
        sum(
            jnp.dot(r, w, preferred_element_type=jnp.float32)
            for r, w in zip(row_chunks, value_blocks)
        )
        + adapter_scale * jnp.dot(value_reduced, value_up_map, preferred_element_type=jnp.float32)
    ).astype(jnp.bfloat16)
    value_rows_all = jnp.concatenate(gather_blocks(values_local), axis=0)

    key_rank = jnp.arange(seq_size * keys_dev, dtype=jnp.int32)
    key_owner = seq_index ^ (key_rank // keys_dev)
    doc_ends = jnp.cumsum(document_slots)
    offset = key_rank % keys_dev
    is_context = offset < tok_dev
    key_unit = jnp.where(
        is_context, (key_owner * tok_dev + offset) // 4, key_owner * slot_dev + offset - tok_dev
    )
    key_doc = doc_index(key_unit, doc_ends)
    slot_unit = seq_index * slot_dev + jnp.arange(slot_dev, dtype=jnp.int32)
    row_unit = jnp.repeat(slot_unit, group_heads)
    row_doc = doc_index(row_unit, doc_ends)
    allowed = (key_doc[None, :] == row_doc[:, None]) & (
        is_context[None, :] | (key_unit[None, :] <= row_unit[:, None])
    )
    score_scale = head_dim ** (-0.5)
    query_rows = query_rows_out.reshape(slot_dev * group_heads, head_dim)
    scores = jnp.where(allowed, trailing_contract(query_rows, keys_all) * score_scale, mask_fill)
    row_top = jnp.max(scores, axis=1, keepdims=True)
    exponent = jnp.exp(scores - row_top)
    probability = exponent / jnp.sum(exponent, axis=1, keepdims=True)
    prob_low = probability.astype(jnp.bfloat16)
    attended = (
        jnp.dot(prob_low, value_rows_all, preferred_element_type=jnp.float32)
        .reshape(slot_dev, group_heads * head_dim)
        .astype(jnp.bfloat16)
    )
    slots_all = jnp.concatenate(gather_blocks(attended), axis=0)
    partial = jnp.dot(slots_all, output_weight, preferred_element_type=jnp.float32)
    total_slots = slot_dev * seq_size
    half = total_slots // 2
    odd = section_index % 2
    mine = lax.dynamic_slice_in_dim(partial, odd * half, half, 0)
    other = lax.dynamic_slice_in_dim(partial, (1 - odd) * half, half, 0)
    mine = mine + swap(other.astype(jnp.bfloat16), "section", 1).astype(jnp.float32)
    mine_low = mine.astype(jnp.bfloat16)
    for far in range(2, section_extent, 2):
        mine = mine + swap(mine_low, "section", far).astype(jnp.float32)
    mine_low = mine.astype(jnp.bfloat16)
    other_low = swap(mine_low, "section", 1)
    hidden = jnp.concatenate(
        [jnp.where(odd == 0, mine_low, other_low), jnp.where(odd == 0, other_low, mine_low)],
        axis=0,
    ).astype(jnp.float32)

    weighted = total_slots ** (-0.5) * gradient_rows.astype(jnp.float32) * decoder_gain[None, :]
    local_sums = jnp.stack(
        [jnp.sum(hidden * hidden, axis=1), jnp.sum(weighted * hidden, axis=1)]
    )
    ordered_sums = jnp.concatenate(
        in_order(jnp.split(local_sums, seq_size, axis=1), seq_index), axis=1
    )
    sums = ordered_sums
    for bits in range(1, seq_size):
        sums = sums + swap(ordered_sums, "seq", bits)
    sums = jnp.concatenate(in_order(jnp.split(sums, seq_size, axis=1), seq_index), axis=1)
    square_sum, cross_sum = sums[0], sums[1]
    inv_rms = lax.rsqrt(square_sum / model_width + epsilon)
    normed_all = (hidden * inv_rms[:, None] * decoder_gain[None, :]).astype(jnp.bfloat16)
    owners = seq_size // section_extent
    normed = jnp.concatenate(
        [
            lax.dynamic_slice_in_dim(
                normed_all, ((section_index * owners + i) ^ seq_index) * slot_dev, slot_dev, 0
            )
            for i in range(owners)
        ],
        axis=0,
    )
    d_hidden = (
        inv_rms[:, None] * weighted - hidden * (inv_rms**3 * cross_sum / model_width)[:, None]
    ).astype(jnp.bfloat16)
    d_attended = scatter_sum(
        jnp.split(trailing_contract(d_hidden, output_weight), seq_size, axis=0)
    ).astype(jnp.bfloat16)

    grad_rows_local = d_attended.reshape(slot_dev * group_heads, head_dim)
    value_gradient = scatter_sum(
        jnp.split(leading_contract(prob_low, grad_rows_local), seq_size, axis=0)
    ).astype(jnp.bfloat16)
    d_probs = trailing_contract(grad_rows_local, value_rows_all)
    center = jnp.sum(probability * d_probs, axis=1, keepdims=True)
    d_scores = (probability * (d_probs - center)).astype(jnp.bfloat16)
    query_gradient = (
        (score_scale * jnp.dot(d_scores, keys_all, preferred_element_type=jnp.float32))
        .reshape(slot_dev, group_heads * head_dim)
        .astype(jnp.bfloat16)
    )
    query_backward = section_sum(
        adapter_scale * trailing_contract(query_gradient, query_up_map)
    ).astype(jnp.bfloat16)
    query_gradient_all = jnp.concatenate(in_order(gather_blocks(query_gradient), seq_index), axis=0)
    query_up_gradient = adapter_scale * leading_contract(query_reduced_all, query_gradient_all)

    value_backward = section_sum(
        adapter_scale * trailing_contract(value_gradient, value_up_map)
    ).astype(jnp.bfloat16)
    value_up_portion = adapter_scale * leading_contract(value_reduced, value_gradient)
    rank_rows = rank // seq_size
    value_up_mine = lax.dynamic_slice_in_dim(value_up_portion, seq_index * rank_rows, rank_rows, 0)
    for k in range(1, seq_size):
        value_up_mine = value_up_mine + swap(
            lax.dynamic_slice_in_dim(
                value_up_portion, (seq_index ^ k) * rank_rows, rank_rows, 0
            ),
            "seq",
            k,
        )
    value_up_blocks = [value_up_mine] + [swap(value_up_mine, "seq", k) for k in range(1, seq_size)]
    value_up_gradient = jnp.concatenate(in_order(value_up_blocks, seq_index), axis=0)

    section_columns = model_width // section_extent
    own_columns = section_columns // seq_size
    query_parts, value_parts = [], []
    for k in range(seq_size):
        start = section_index * section_columns + (seq_index ^ k) * own_columns
        memory_cols = lax.dynamic_slice_in_dim(memory, start, own_columns, 1)
        context_cols = lax.dynamic_slice_in_dim(context, start, own_columns, 1)
        query_parts.append(leading_contract(memory_cols, query_backward))
        value_parts.append(
            leading_contract(context_cols, value_backward[:tok_dev])
            + leading_contract(memory_cols, value_backward[tok_dev:])
        )
    grad_qa = scatter_sum(query_parts)
    grad_va = scatter_sum(value_parts)
    return (normed, grad_qa, grad_va, query_up_gradient, value_up_gradient)


def solution(mesh):
    in_specs = (
        P("seq", None),
        P("seq", None),
        P(None, "section"),
        P("seq", "section"),
        P("seq", "section"),
        P(),
        P(None, "section"),
        P("seq", None),
        P(None, "section"),
        P("section", "seq"),
        P("seq"),
        P(),
        P("section", "seq"),
    )
    out_specs = (
        P("section", "seq"),
        P(("section", "seq"), None),
        P(("section", "seq"), None),
        P(None, "section"),
        P(None, "section"),
    )
    return jax.shard_map(body, mesh=mesh, in_specs=in_specs, out_specs=out_specs, check_vma=False)
```
